32 devices in a mesh: beam: 2 (over y), freq: 8 (over z, x), tm: 2 (over core).
Axes of the slice: x: 2, y: 2, z: 4, core: 2. Of those that a mesh axis runs over, the one named last changes fastest.
Arguments:
- spectra: float32 [256, 16384], P(('beam', 'freq'), 'tm'), parts along dimension 0, may hold values from -250 to 250
- local_delays: int32 [4, 3, 128], P(None, None, 'freq'), may hold values from 0 to 8, as said below
- merge_delays: int32 [3, 3, 128], P(None, None, 'freq'), may hold values from 0 to 64, as said below
- widths: int32 [16], replicated, may hold values from 1 to 32, as said below
Outputs:
- detections: float32 [256, 16384], P(('beam', 'freq'), 'tm'), parts along dimension 0
The draws below stay inside these ranges and needn't reach their ends.
There are 2 independent parts, one for each index of `beam`. The reference program is written for one: setup_inputs(seed, part) draws one part's arguments, and reference() takes and returns one part's arrays. A program takes and returns all parts, laid end to end along the dimension named above; an argument that names none is the same for every part. Nothing has to cross between parts.
Inputs may be any that keep to these rules, and one draw needn't show every extreme that they name: `local_delays`: entries [s, 0, r] and [s, 1, r] lie in 0 to 2**s - 1, entry [s, 2, r] in 0 to 2**s, and [s, 2, 0] equals 2**s. `merge_delays`: entries [j, 0, r] and [j, 1, r] lie in 0 to 15, entry [j, 2, r] in 0 to 16 * 2**j, and [j, 2, 0] equals 16 * 2**j. 16 distinct widths, one of them 32.
All inputs are finite; a program needn't handle non-finite values.
Results may differ from the reference program's by a relative error of at most 0.00002.
Values sent between devices are 32-bit elements; how exact they have to be, the bound alone decides.
A program may use at most 64 MiB of HBM per device.

```python
import math
import jax
import jax.numpy as jnp
from jax import lax

CH_DEV = 16
LLEVELS = 4
BLEVELS = 3
CHANNELS = 128
TIMES = 16384
WMAX = 32
NWIDTH = 16


def draw_spectra(key, part):
    subkeys = jax.random.split(key, 3)
    fraction = jnp.arange(TIMES, dtype=jnp.float32) / TIMES
    noise_part = jnp.clip(jax.random.normal(subkeys[0], (CHANNELS, TIMES), jnp.float32), -5.0, 5.0)
    channel_gain = jnp.exp(jax.random.uniform(subkeys[1], (CHANNELS, 1), jnp.float32, 0.0, math.log(10.0)))
    baseline = jax.random.uniform(subkeys[2], (CHANNELS, 1), jnp.float32, -2.0, 2.0)
    return channel_gain * (noise_part * (0.5 + fraction) + baseline * 3.0 * fraction)


def draw_local_delays(key, part):
    subkeys = jax.random.split(key, 3)
    level_size = (2 ** jnp.arange(LLEVELS, dtype=jnp.int32))[:, None]
    low_pick = jax.random.randint(subkeys[0], (LLEVELS, CHANNELS), 0, level_size)
    high_pick = jax.random.randint(subkeys[1], (LLEVELS, CHANNELS), 0, level_size)
    lag_table = jax.random.randint(subkeys[2], (LLEVELS, CHANNELS), 0, level_size + 1)
    lag_table = lag_table.at[:, 0].set(level_size[:, 0])
    return jnp.stack([low_pick, high_pick, lag_table], axis=1).astype(jnp.int32)


def draw_merge_delays(key, part):
    subkeys = jax.random.split(key, 3)
    level_size = (CH_DEV * 2 ** jnp.arange(BLEVELS, dtype=jnp.int32))[:, None]
    low_pick = jax.random.randint(subkeys[0], (BLEVELS, CHANNELS), 0, CH_DEV)
    high_pick = jax.random.randint(subkeys[1], (BLEVELS, CHANNELS), 0, CH_DEV)
    lag_table = jax.random.randint(subkeys[2], (BLEVELS, CHANNELS), 0, level_size + 1)
    lag_table = lag_table.at[:, 0].set(level_size[:, 0])
    return jnp.stack([low_pick, high_pick, lag_table], axis=1).astype(jnp.int32)


def draw_widths(key, part):
    shuffled = jax.random.permutation(key, WMAX - 1) + 1
    return jnp.concatenate([shuffled[:NWIDTH - 1], jnp.array([WMAX])]).astype(jnp.int32)


def setup_inputs(seed: int = 0, part: int = 0) -> dict:
    splits = jax.random.split(jax.random.key(seed), 5)
    part_keys = jax.random.split(jax.random.fold_in(splits[4], part), 5)
    return {
        "spectra": draw_spectra(jax.random.fold_in(jax.random.fold_in(splits[4], part), 71), part),
        "local_delays": draw_local_delays(jax.random.fold_in(splits[4], 71), part),
        "merge_delays": draw_merge_delays(jax.random.fold_in(splits[4], 71), part),
        "widths": draw_widths(jax.random.fold_in(splits[4], 71), part),
    }


EPSILON = 1e-05

def shift_rows(signal, delays, length):
    return jax.vmap(lambda one_row, one_lag: lax.dynamic_slice_in_dim(one_row, one_lag, length))(signal, delays)

def reference(spectra, local_delays, merge_delays, widths):
    average = lax.optimization_barrier(jnp.mean(spectra, axis=1, keepdims=True))
    centered = spectra - average
    variance = lax.optimization_barrier(jnp.mean(centered * centered, axis=1, keepdims=True))
    series = centered / jnp.sqrt(variance + EPSILON)
    row_ids = jnp.arange(CHANNELS, dtype=jnp.int32)
    for level_num in range(LLEVELS):
        level_size = 2 ** level_num
        base_row = row_ids // (2 * level_size) * (2 * level_size)
        low_rows = series[base_row + local_delays[level_num, 0]]
        high_rows = jnp.pad(series[base_row + level_size + local_delays[level_num, 1]], ((0, 0), (0, level_size)))
        series = low_rows + shift_rows(high_rows, local_delays[level_num, 2], TIMES)
    device_ids = row_ids // CH_DEV
    for level_num in range(BLEVELS):
        stride = 2 ** level_num
        low_device = device_ids - device_ids // stride % 2 * stride
        low_rows = series[low_device * CH_DEV + merge_delays[level_num, 0]]
        high_rows = series[(low_device + stride) * CH_DEV + merge_delays[level_num, 1]]
        high_rows = jnp.pad(high_rows, ((0, 0), (0, CH_DEV * stride)))
        series = low_rows + shift_rows(high_rows, merge_delays[level_num, 2], TIMES)
    extended = jnp.pad(series, ((0, 0), (0, WMAX - 1)))
    running = jnp.zeros((CHANNELS, TIMES), jnp.float32)
    strongest = jnp.full((CHANNELS, TIMES), -jnp.inf, jnp.float32)
    for offset in range(WMAX):
        running = running + extended[:, offset:offset + TIMES]
        chosen = jnp.any(widths == offset + 1)
        strongest = jnp.where(chosen, jnp.maximum(strongest, running * (1.0 / math.sqrt(offset + 1))), strongest)
    return strongest * (1.0 / math.sqrt(CHANNELS))
```

```python
import functools
import math

import jax
import jax.numpy as jnp
from jax import lax
from jax.experimental import pallas as pl
from jax.experimental.pallas import tpu as pltpu
from jax.sharding import PartitionSpec as P

WMAX = 32
EPSILON = 1e-05
LANES = 128
SUB = 8
MESH = pl.DeviceIdType.MESH
FIRST_LAG = 1
MID_LAG = 1
LAST_LAG = 3
UNROLL = 16
MAX_SPLIT = 2


def flip(value, mask):
    bit = 1
    while bit <= mask:
        if mask & bit:
            value = value + bit - 2 * bit * ((value // bit) % 2)
        bit *= 2
    return value


def kernel(geo, names, x_ref, ld_ref, md_ref, w_ref, o_ref, *scratch):
    channels, chunks, freq_count, halo_chunks, split = geo
    ref = dict(zip(names, scratch))
    sets = 2**split
    groups = channels // SUB
    llevels = channels.bit_length() - 1
    flevels = freq_count.bit_length() - 1
    blevels = flevels - split
    samples = chunks * LANES
    block = chunks // sets
    count = block // SUB
    lowest = freq_count // sets
    nwidth = w_ref.shape[0]
    xv, st_own, st_peer, pack, hpeer = (ref[n] for n in ("xv", "st_own", "st_peer", "pack", "hpeer"))
    fin, tri, scl = ref["fin"], ref["tri"], ref["scl"]

    tm = lax.axis_index("tm")
    freq = lax.axis_index("freq")
    k = freq // lowest
    f0 = freq % lowest
    peer = {"tm": 1 - tm}
    zs = [flip(k, m) for m in range(sets)]
    same = [{"freq": zs[m] * lowest + f0} for m in range(sets)]
    cross = [{"freq": zs[m] * lowest + f0, "tm": 1 - tm} for m in range(sets)]
    sides = [(freq // 2**j) % 2 for j in range(blevels)]
    partners = [{"freq": flip(freq, 2**j)} for j in range(blevels)]
    remote = [m for m in RAW_ORDER if m < sets] if sets > 1 else []

    barrier = pltpu.get_barrier_semaphore()
    others = [peer] + partners + [same[m] for m in remote] + [cross[m] for m in remote]
    for other in others:
        pl.semaphore_signal(barrier, inc=1, device_id=other, device_id_type=MESH)

    c0_of = [block - SUB * (p + 1) for p in range(count)]

    def rows_of(first, size):
        return pl.ds(pl.multiple_of(first * SUB, SUB), size * SUB)

    load_x = pltpu.make_async_copy(x_ref, xv, ref["lsem"].at[0])
    load_x.start()
    own_loads = []
    for p in range(count):
        own_loads.append(pltpu.make_async_copy(
            x_ref.at[:, rows_of(k * block + c0_of[p], SUB), :], ref["raw", 0, p], ref["osem"].at[p],
        ))
    own_halo = pltpu.make_async_copy(
        x_ref.at[:, rows_of(jnp.minimum((k + 1) * block, chunks - halo_chunks), halo_chunks), :],
        ref["rawh", 0], ref["lsem"].at[1],
    )
    for copy in own_loads + [own_halo]:
        copy.start()

    sent = []

    def push(src, dst, ssem, rsem, device):
        copy = pltpu.make_async_remote_copy(
            src_ref=src, dst_ref=dst, send_sem=ssem, recv_sem=rsem,
            device_id=device, device_id_type=MESH,
        )
        sent.append(copy)
        return copy

    peer_halo = push(
        x_ref.at[:, pl.ds(0, halo_chunks * SUB), :], hpeer,
        ref["psem"].at[0], ref["psem"].at[1], peer,
    )
    stat_copy = push(st_own, st_peer, ref["psem"].at[2], ref["psem"].at[3], peer)
    raw_copies, halo_copies, pack_copies, table_copies = {}, {}, {}, {}
    for m in remote:
        last = zs[m] == sets - 1
        halo_copies[m] = push(
            x_ref.at[:, rows_of(jnp.where(last, 0, (zs[m] + 1) * block), halo_chunks), :],
            ref["rawh", m], ref["hsend"].at[m], ref["hrecv"].at[m],
            {"freq": zs[m] * lowest + f0, "tm": jnp.where(last, 1 - tm, tm)},
        )
        for p in range(count):
            raw_copies[p, m] = push(
                x_ref.at[:, rows_of(zs[m] * block + c0_of[p], SUB), :], ref["raw", m, p],
                ref["rsend"].at[p, m], ref["rrecv"].at[p, m], same[m],
            )
        pack_copies[m] = push(
            pack, ref["pack", m], ref["ksend"].at[m], ref["krecv"].at[m], same[m],
        )
        table_copies[m] = [
            push(ld_ref, ref["ld", m], ref["tsend"].at[0, m], ref["trecv"].at[0, m], same[m]),
            push(md_ref, ref["md", m], ref["tsend"].at[1, m], ref["trecv"].at[1, m], same[m]),
        ]

    pl.semaphore_wait(barrier, len(others))
    for m in remote:
        halo_copies[m].start()
        raw_copies[0, m].start()
    peer_halo.start()

    lane = lax.broadcasted_iota(jnp.int32, (SUB, LANES), 1)
    load_x.wait()
    for g in range(groups):
        data = xv[g].reshape(chunks, SUB, LANES)
        mean = jnp.sum(jnp.sum(data, axis=0), axis=1, keepdims=True) / samples
        off = data - mean[None]
        square = jnp.sum(jnp.sum(off * off, axis=0), axis=1, keepdims=True)
        st_own[0, pl.ds(g * SUB, SUB), :] = jnp.broadcast_to(mean, (SUB, LANES))
        st_own[1, pl.ds(g * SUB, SUB), :] = jnp.broadcast_to(square, (SUB, LANES))
    stat_copy.start()
    for m in remote:
        for copy in table_copies[m]:
            copy.start()

    before = lax.broadcasted_iota(jnp.int32, (LANES, 2 * LANES), 0)
    after = lax.broadcasted_iota(jnp.int32, (LANES, 2 * LANES), 1)
    tri[...] = jnp.where(before < after, 1.0, 0.0)
    norm = 1.0 / math.sqrt(channels * freq_count)
    for i in range(nwidth):
        wide = jnp.full((SUB, LANES), w_ref[i].astype(jnp.float32), jnp.float32)
        scl[i] = (1.0 / jnp.sqrt(wide)) * norm

    stat_copy.wait_recv()
    mean_a, mean_b = st_own[0], st_peer[0]
    gap = mean_a - mean_b
    variance = (st_own[1] + st_peer[1] + gap * gap * (samples / 2)) / (2 * samples)
    mean_all = (mean_a + mean_b) * 0.5
    gain_all = 1.0 / jnp.sqrt(variance + EPSILON)
    ref["nrm", 0][0] = mean_all
    ref["nrm", 0][1] = gain_all
    wide = LANES // (2 * groups)
    packed = gain_all[(groups - 1) * SUB :]
    for g in reversed(range(groups)):
        if g < groups - 1:
            packed = jnp.where(lane < (2 * g + 2) * wide, gain_all[g * SUB : (g + 1) * SUB], packed)
        packed = jnp.where(lane < (2 * g + 1) * wide, mean_all[g * SUB : (g + 1) * SUB], packed)
    if remote:
        pack[...] = packed
    for m in remote:
        pack_copies[m].start()
    for p in range(1, count):
        for m in remote:
            raw_copies[p, m].start()

    keep = jnp.where((tm == 1) & (k == sets - 1), 0.0, 1.0)
    halo_size = -(-halo_chunks // SUB) * SUB

    def side_of(m, i):
        bit = (k // 2**i) % 2
        return 1 - bit if (m >> i) & 1 else bit

    def source(level, p, m):
        if level < blevels:
            return ref["bf", level, p, m], c0_of[p]
        i = level - blevels
        return ref["pb", i, m & ~(1 << i)], 0

    def put(level, p, m, r, c0, size, value):
        buf, first = source(level, p, m)
        side = sides[level] if level < blevels else side_of(m, level - blevels)
        buf[side, r, pl.ds(c0 - first, size), :] = value

    def rows(body):
        for g in range(groups):
            body(g)

    def tiles(p):
        found = [(c0_of[p], SUB, False)]
        if p == 0:
            found.insert(0, (block, halo_size, True))
        return found

    def normalise(p, m, c0, size, is_halo):
        nrm = ref["nrm", m]

        def body(g):
            out = []
            for i in range(SUB):
                r = g * SUB + i
                gain = nrm[1, pl.ds(r, 1), :]
                if is_halo:
                    part = ref["rawh", m][g, pl.ds(i, halo_chunks, stride=SUB), :]
                    if m == 0:
                        part = jnp.where(
                            k == sets - 1, hpeer[g, pl.ds(i, halo_chunks, stride=SUB), :], part,
                        )
                    gain = gain * keep
                else:
                    part = ref["raw", m, p][g, pl.ds(i, size, stride=SUB), :]
                out.append((part - nrm[0, pl.ds(r, 1), :]) * gain)
            for i in range(SUB):
                n = halo_chunks if is_halo else size
                ref["loc", 0, m][g * SUB + i, pl.ds(c0, n), :] = out[i]

        rows(body)

    def merged(low, high, lag, span, c0, size):
        if span < LANES:
            jump = 0
        else:
            jump = lag // LANES
            lag = lag % LANES
        cur = high(c0 + jump, size)
        nxt = high(c0 + jump + 1, size)
        lanes = lax.broadcasted_iota(jnp.int32, (size, LANES), 1)
        mixed = jnp.where(lanes < lag, nxt, cur)
        return low(c0, size) + pltpu.roll(mixed, (LANES - lag) % LANES, 1)

    def local_level(s, p, m, c0, size):
        span = 2**s
        src = ref["loc", s, m]
        table = ref["ld", m] if m else ld_ref

        def body(g):
            out = []
            for i in range(SUB):
                r = g * SUB + i
                base = (r // (2 * span)) * (2 * span)
                lo_row = base + table[0, s, r]
                hi_row = base + span + table[1, s, r]
                out.append(merged(
                    lambda c, n: src[lo_row, pl.ds(c, n), :],
                    lambda c, n: src[hi_row, pl.ds(c, n), :],
                    table[2, s, r], span, c0, size,
                ))
            for i in range(SUB):
                r = g * SUB + i
                if s + 1 < llevels:
                    ref["loc", s + 1, m][r, pl.ds(c0, size), :] = out[i]
                else:
                    put(0, p, m, r, c0, size, out[i])

        rows(body)

    def merge_level(j, p, m, c0, size):
        span = channels * 2**j
        src, first = source(j, p, m)
        table = ref["md", m] if m else md_ref

        def body(g):
            out = []
            for i in range(SUB):
                r = g * SUB + i
                lo_row = table[j, 0, r]
                hi_row = table[j, 1, r]
                out.append(merged(
                    lambda c, n: src[0, lo_row, pl.ds(c, n), :],
                    lambda c, n: src[1, hi_row, pl.ds(c, n), :],
                    table[j, 2, r], span, c0 - first, size,
                ))
            for i in range(SUB):
                r = g * SUB + i
                if j + 1 < flevels:
                    put(j + 1, p, m, r, c0, size, out[i])
                else:
                    fin[pl.ds(r * SUB, SUB), :] = out[i]

        rows(body)

    def prefix(m, c0):
        sums = jnp.dot(
            fin[...], tri[...], precision=lax.Precision.HIGHEST,
            preferred_element_type=jnp.float32,
        )
        own = sums[:, :LANES].reshape(channels, SUB, LANES)
        ref["eb", m][:, pl.ds(c0, SUB), :] = own
        return own, sums[:, LANES:].reshape(channels, SUB, LANES)

    def boxcar(p, m, c0):
        own, total = prefix(m, c0)
        far = total + ref["eb", m][:, pl.ds(c0 + 1, SUB), :]
        lanes = lax.broadcasted_iota(jnp.int32, (channels, SUB, LANES), 2)

        def body(at, best):
            for u in range(unroll):
                i = at * unroll + u
                wide = w_ref[i]
                mixed = jnp.where(lanes < wide, far, own)
                ahead = pltpu.roll(mixed, LANES - wide, 2)
                best = jnp.maximum(best, (ahead - own) * scl[i][None])
            return best

        unroll = math.gcd(nwidth, UNROLL)
        best = lax.fori_loop(
            0, nwidth // unroll, body, jnp.full((channels, SUB, LANES), -jnp.inf, jnp.float32)
        )
        for r in range(channels):
            g, i = r // SUB, r % SUB
            if m:
                ref["res", p, m][g, pl.ds(i, SUB, stride=SUB), :] = best[r]
            else:
                at = pl.multiple_of((k * block + c0) * SUB, SUB) + i
                o_ref[g, pl.ds(at, SUB, stride=SUB), :] = best[r]

    level_copies = {}
    for j in range(blevels):
        for p in range(count):
            for m in range(sets):
                size = SUB + (halo_chunks if p == 0 else 0)
                window = ref["bf", j, p, m].at[sides[j], :, pl.ds(0, size), :]
                level_copies[j, p, m] = push(
                    window, window, ref["bsend"].at[j, p, m], ref["brecv"].at[j, p, m], partners[j],
                )
    result_copies = {}
    for p in range(count):
        for m in remote:
            result_copies[p, m] = push(
                ref["res", p, m], o_ref.at[:, rows_of(k * block + c0_of[p], SUB), :],
                ref["osend"].at[p, m], ref["orecv"].at[p, m], same[m],
            )

    def local_stage(p, m):
        if m:
            if p == 0:
                for copy in [halo_copies[m], pack_copies[m]] + table_copies[m]:
                    copy.wait_recv()
                got = ref["pack", m][...]
                for g in range(groups):
                    for i in range(2):
                        at = (2 * g + i) * wide
                        ref["nrm", m][i, pl.ds(g * SUB, SUB), :] = jnp.broadcast_to(
                            got[:, at : at + 1], (SUB, LANES)
                        )
            raw_copies[p, m].wait_recv()
        else:
            if p == 0:
                own_halo.wait()
                peer_halo.wait_recv()
            own_loads[p].wait()
        for c0, size, is_halo in tiles(p):
            normalise(p, m, c0, size, is_halo)
            for s in range(llevels):
                local_level(s, p, m, c0, size)
        if blevels:
            level_copies[0, p, m].start()

    def merge_stage(j, p, m):
        if j < blevels:
            level_copies[j, p, m].wait_recv()
            if p:
                over = channels * 2**j // LANES + 1
                ref["bf", j, p, m][:, :, pl.ds(SUB, over), :] = ref["bf", j, p - 1, m][:, :, pl.ds(0, over), :]
        for c0, size, is_halo in tiles(p):
            if j + 1 < flevels:
                merge_level(j, p, m, c0, size)
            elif is_halo:
                merge_level(j, p, m, c0, SUB)
                prefix(m, c0)
            else:
                merge_level(j, p, m, c0, SUB)
                boxcar(p, m, c0)
        if j + 1 < blevels:
            level_copies[j + 1, p, m].start()
        if j + 1 == flevels and m:
            result_copies[p, m].start()

    if split == 0:
        lags = [FIRST_LAG] + [MID_LAG] * (flevels - 2) + [LAST_LAG]
        behind = [sum(lags[: j + 1]) for j in range(flevels)]
        for step in range(count + behind[-1]):
            if step < count:
                local_stage(step, 0)
            for j in range(flevels):
                if 0 <= step - behind[j] < count:
                    merge_stage(j, step - behind[j], 0)
    else:
        arrive = [m for m in LOCAL_ORDER if m < sets]
        leave = [m for m in LEAVE_ORDER if m < sets]
        local_stage(0, 0)
        local_stage(1, 0)
        for m in arrive:
            local_stage(0, m)
        for p in range(count):
            for j in range(flevels - 1):
                for m in [0] + arrive:
                    merge_stage(j, p, m)
            ready = list(arrive) if p + 1 < count else []
            for m in leave:
                merge_stage(flevels - 1, p, m)
                if ready:
                    local_stage(p + 1, ready.pop(0))
            for m in ready:
                local_stage(p + 1, m)
            if p + 2 < count:
                local_stage(p + 2, 0)
            merge_stage(flevels - 1, p, 0)

    for copy in result_copies.values():
        copy.wait_recv()
    for copy in sent:
        copy.wait_send()


RAW_ORDER = (3, 2, 1)
LOCAL_ORDER = (1, 3, 2)
LEAVE_ORDER = (3, 2, 1)


def per_device(mesh_shape, spectra, local_delays, merge_delays, widths):
    channels, block_len = spectra.shape
    freq_count = mesh_shape["freq"]
    chunks = block_len // LANES
    groups = channels // SUB
    halo_chunks = -(-(channels * freq_count - 1 + LANES) // LANES)
    llevels = channels.bit_length() - 1
    flevels = freq_count.bit_length() - 1
    split = 0
    while (
        split < min(MAX_SPLIT, flevels)
        and chunks % (SUB * 2 ** (split + 2)) == 0
        and 4 * halo_chunks <= chunks // 2 ** (split + 1)
    ):
        split += 1
    sets = 2**split
    block = chunks // sets
    count = block // SUB
    blevels = flevels - split
    halo_size = -(-halo_chunks // SUB) * SUB
    over = -(-(channels * freq_count // 2 // LANES + 1) // SUB) * SUB
    depth = block + halo_size + SUB
    f32 = jnp.float32
    flat = spectra.reshape(groups, SUB, chunks, LANES).transpose(0, 2, 1, 3)
    flat = flat.reshape(groups, chunks * SUB, LANES)
    dma = pltpu.SemaphoreType.DMA

    def vmem(*shape):
        return pltpu.VMEM(shape, f32)

    scratch = {
        "xv": vmem(*flat.shape),
        "st_own": vmem(2, channels, LANES),
        "st_peer": vmem(2, channels, LANES),
        "pack": vmem(SUB, LANES),
        "hpeer": vmem(groups, halo_chunks * SUB, LANES),
        "fin": vmem(channels * SUB, LANES),
        "tri": vmem(LANES, 2 * LANES),
        "scl": vmem(widths.shape[0], SUB, LANES),
        "lsem": dma((2,)),
        "osem": dma((count,)),
        "psem": dma((4,)),
        "hsend": dma((sets,)),
        "hrecv": dma((sets,)),
        "ksend": dma((sets,)),
        "krecv": dma((sets,)),
        "tsend": dma((2, sets)),
        "trecv": dma((2, sets)),
        "rsend": dma((count, sets)),
        "rrecv": dma((count, sets)),
        "osend": dma((count, sets)),
        "orecv": dma((count, sets)),
    }
    if blevels:
        scratch["bsend"] = dma((blevels, count, sets))
        scratch["brecv"] = dma((blevels, count, sets))
    for m in range(sets):
        scratch["rawh", m] = vmem(groups, halo_chunks * SUB, LANES)
        scratch["nrm", m] = vmem(2, channels, LANES)
        scratch["eb", m] = vmem(channels, depth, LANES)
        for s in range(llevels):
            scratch["loc", s, m] = vmem(channels, depth, LANES)
        for p in range(count):
            scratch["raw", m, p] = vmem(groups, SUB * SUB, LANES)
            tail = (halo_size if p == 0 else 0) + over
            for j in range(blevels):
                scratch["bf", j, p, m] = vmem(2, channels, SUB + tail, LANES)
            if m:
                scratch["res", p, m] = vmem(groups, SUB * SUB, LANES)
        for i in range(split):
            if not (m >> i) & 1:
                scratch["pb", i, m] = vmem(2, channels, block + halo_size + over, LANES)
        if m:
            scratch["pack", m] = vmem(SUB, LANES)
            scratch["ld", m] = pltpu.SMEM((3, llevels, channels), jnp.int32)
            scratch["md", m] = pltpu.SMEM((flevels, 3, channels), jnp.int32)

    smem = pl.BlockSpec(memory_space=pltpu.SMEM)
    geo = (channels, chunks, freq_count, halo_chunks, split)
    out = pl.pallas_call(
        functools.partial(kernel, geo, tuple(scratch)),
        out_shape=pltpu.VMEM(flat.shape, f32),
        in_specs=[pl.BlockSpec(memory_space=pl.ANY), smem, smem, smem],
        out_specs=pl.BlockSpec(memory_space=pltpu.VMEM),
        scratch_shapes=list(scratch.values()),
        compiler_params=pltpu.CompilerParams(
            collective_id=0, has_side_effects=True, vmem_limit_bytes=56 * 2**20
        ),
    )(flat, local_delays.transpose(1, 0, 2), merge_delays, widths)
    out = out.reshape(groups, chunks, SUB, LANES).transpose(0, 2, 1, 3)
    return out.reshape(channels, block_len)


def solution(mesh):
    placed = (P(("beam", "freq"), "tm"), P(None, None, "freq"), P(None, None, "freq"), P())
    return jax.shard_map(
        functools.partial(per_device, dict(mesh.shape)), mesh=mesh, in_specs=placed,
        out_specs=P(("beam", "freq"), "tm"), check_vma=False,
    )
```

```python
import functools
import math

import jax
import jax.numpy as jnp
from jax import lax
from jax.experimental import pallas as pl
from jax.experimental.pallas import tpu as pltpu
from jax.sharding import PartitionSpec as P

WMAX = 32
EPSILON = 1e-05
LANES = 128
SUB = 8
MESH = pl.DeviceIdType.MESH
RAW_ORDER = (3, 2, 1)
LOCAL_ORDER = (1, 3, 2)
LEAVE_ORDER = (2, 3, 1)
DOWN_ORDER = (3, 2, 1)
DOWN_FIRST = 1
UP_ORDER = (1, 2, 3)
INNER_AT = -1
OUTER_AT = 2
NEXT_AT = 1
FIRST_LAG = 1
MID_LAG = 1
LAST_LAG = 3
UNROLL = 16
MAX_SPLIT = 2


def flip(value, mask):
    bit = 1
    while bit <= mask:
        if mask & bit:
            value = value + bit - 2 * bit * ((value // bit) % 2)
        bit *= 2
    return value


def kernel(geo, names, x_ref, ld_ref, md_ref, w_ref, o_ref, *scratch):
    channels, chunks, freq_count, halo_chunks, split = geo
    ref = dict(zip(names, scratch))
    sets = 2**split
    groups = channels // SUB
    llevels = channels.bit_length() - 1
    flevels = freq_count.bit_length() - 1
    blevels = flevels - split
    samples = chunks * LANES
    block = chunks // sets
    count = block // SUB
    lowest = freq_count // sets
    nwidth = w_ref.shape[0]
    xv, st_own, st_peer, pack, hpeer = (ref[n] for n in ("xv", "st_own", "st_peer", "pack", "hpeer"))
    fin, tri, scl = ref["fin"], ref["tri"], ref["scl"]

    tm = lax.axis_index("tm")
    freq = lax.axis_index("freq")
    k = freq // lowest
    f0 = freq % lowest
    peer = {"tm": 1 - tm}
    zs = [flip(k, m) for m in range(sets)]
    same = [{"freq": zs[m] * lowest + f0} for m in range(sets)]
    cross = [{"freq": zs[m] * lowest + f0, "tm": 1 - tm} for m in range(sets)]
    sides = [(freq // 2**j) % 2 for j in range(blevels)]
    partners = [{"freq": flip(freq, 2**j)} for j in range(blevels)]
    remote = [m for m in RAW_ORDER if m < sets] if sets > 1 else []

    barrier = pltpu.get_barrier_semaphore()
    for other in [peer] + partners:
        pl.semaphore_signal(barrier, inc=1, device_id=other, device_id_type=MESH)
    for m in remote:
        @pl.when(zs[m] > k)
        def _(m=m):
            for other in (same[m], cross[m]):
                pl.semaphore_signal(barrier, inc=1, device_id=other, device_id_type=MESH)

    c0_of = [block - SUB * (p + 1) for p in range(count)]

    def rows_of(first, size):
        return pl.ds(pl.multiple_of(first * SUB, SUB), size * SUB)

    load_x = pltpu.make_async_copy(x_ref, xv, ref["lsem"].at[0])
    load_x.start()
    own_loads = []
    for p in range(count):
        own_loads.append(pltpu.make_async_copy(
            x_ref.at[:, rows_of(k * block + c0_of[p], SUB), :], ref["raw", 0, p], ref["osem"].at[p],
        ))
    own_halo = pltpu.make_async_copy(
        x_ref.at[:, rows_of(jnp.minimum((k + 1) * block, chunks - halo_chunks), halo_chunks), :],
        ref["rawh", 0], ref["lsem"].at[1],
    )
    for copy in own_loads + [own_halo]:
        copy.start()

    sent = []

    def push(src, dst, ssem, rsem, device):
        copy = pltpu.make_async_remote_copy(
            src_ref=src, dst_ref=dst, send_sem=ssem, recv_sem=rsem,
            device_id=device, device_id_type=MESH,
        )
        sent.append(copy)
        return copy

    peer_halo = push(
        x_ref.at[:, pl.ds(0, halo_chunks * SUB), :], hpeer,
        ref["psem"].at[0], ref["psem"].at[1], peer,
    )
    stat_copy = push(st_own, st_peer, ref["psem"].at[2], ref["psem"].at[3], peer)
    raw_copies, halo_copies, pack_copies, table_copies = {}, {}, {}, {}
    for m in remote:
        last = zs[m] == sets - 1
        halo_copies[m] = push(
            x_ref.at[:, rows_of(jnp.where(last, 0, (zs[m] + 1) * block), halo_chunks), :],
            ref["rawh", m], ref["hsend"].at[m], ref["hrecv"].at[m],
            {"freq": zs[m] * lowest + f0, "tm": jnp.where(last, 1 - tm, tm)},
        )
        for p in range(count):
            raw_copies[p, m] = push(
                x_ref.at[:, rows_of(zs[m] * block + c0_of[p], SUB), :], ref["raw", m, p],
                ref["rsend"].at[p, m], ref["rrecv"].at[p, m], same[m],
            )
        pack_copies[m] = push(
            pack, ref["pack", m], ref["ksend"].at[m], ref["krecv"].at[m], same[m],
        )
        table_copies[m] = [
            push(ld_ref, ref["ld", m], ref["tsend"].at[0, m], ref["trecv"].at[0, m], same[m]),
            push(md_ref, ref["md", m], ref["tsend"].at[1, m], ref["trecv"].at[1, m], same[m]),
        ]

    pl.semaphore_wait(barrier, 1 + blevels + (2 * k if remote else 0))
    for m in remote:
        @pl.when(zs[m] < k)
        def _(m=m):
            for other in (same[m], cross[m]):
                pl.semaphore_signal(ref["ready"].at[m], inc=1, device_id=other, device_id_type=MESH)
    peer_halo.start()

    def start_tables(m):
        for copy in table_copies[m]:
            copy.start()

    def start_first(m):
        halo_copies[m].start()
        raw_copies[0, m].start()

    def at_distance(step, body):
        for m in remote:
            pl.when(zs[m] == k + step)(functools.partial(body, m))

    for step in DOWN_ORDER:
        at_distance(-step, start_tables)
    for step in DOWN_ORDER[:DOWN_FIRST]:
        at_distance(-step, start_first)
    outer = (k == 0) | (k == sets - 1)

    lane = lax.broadcasted_iota(jnp.int32, (SUB, LANES), 1)
    load_x.wait()
    for g in range(groups):
        data = xv[g].reshape(chunks, SUB, LANES)
        mean = jnp.sum(jnp.sum(data, axis=0), axis=1, keepdims=True) / samples
        off = data - mean[None]
        square = jnp.sum(jnp.sum(off * off, axis=0), axis=1, keepdims=True)
        st_own[0, pl.ds(g * SUB, SUB), :] = jnp.broadcast_to(mean, (SUB, LANES))
        st_own[1, pl.ds(g * SUB, SUB), :] = jnp.broadcast_to(square, (SUB, LANES))
    stat_copy.start()

    before = lax.broadcasted_iota(jnp.int32, (LANES, 2 * LANES), 0)
    after = lax.broadcasted_iota(jnp.int32, (LANES, 2 * LANES), 1)
    tri[...] = jnp.where(before < after, 1.0, 0.0)
    norm = 1.0 / math.sqrt(channels * freq_count)
    for i in range(nwidth):
        wide = jnp.full((SUB, LANES), w_ref[i].astype(jnp.float32), jnp.float32)
        scl[i] = (1.0 / jnp.sqrt(wide)) * norm

    stat_copy.wait_recv()
    mean_a, mean_b = st_own[0], st_peer[0]
    gap = mean_a - mean_b
    variance = (st_own[1] + st_peer[1] + gap * gap * (samples / 2)) / (2 * samples)
    mean_all = (mean_a + mean_b) * 0.5
    gain_all = 1.0 / jnp.sqrt(variance + EPSILON)
    ref["nrm", 0][0] = mean_all
    ref["nrm", 0][1] = gain_all
    wide = LANES // (2 * groups)
    packed = gain_all[(groups - 1) * SUB :]
    for g in reversed(range(groups)):
        if g < groups - 1:
            packed = jnp.where(lane < (2 * g + 2) * wide, gain_all[g * SUB : (g + 1) * SUB], packed)
        packed = jnp.where(lane < (2 * g + 1) * wide, mean_all[g * SUB : (g + 1) * SUB], packed)
    if remote:
        pack[...] = packed
    for step in DOWN_ORDER:
        at_distance(-step, lambda m: pack_copies[m].start())
    for step in DOWN_ORDER[DOWN_FIRST:]:
        at_distance(-step, start_first)

    def start_up(m):
        pl.semaphore_wait(ref["ready"].at[m], 2)
        start_tables(m)
        pack_copies[m].start()
        start_first(m)

    for step in UP_ORDER:
        at_distance(step, start_up)

    def start_raw():
        for p in range(1, count):
            for m in remote:
                raw_copies[p, m].start()

    if remote and INNER_AT < 0:
        pl.when(jnp.logical_not(outer))(start_raw)

    keep = jnp.where((tm == 1) & (k == sets - 1), 0.0, 1.0)
    halo_size = -(-halo_chunks // SUB) * SUB

    def side_of(m, i):
        bit = (k // 2**i) % 2
        return 1 - bit if (m >> i) & 1 else bit

    def source(level, p, m):
        if level < blevels:
            return ref["bf", level, p, m], c0_of[p]
        i = level - blevels
        return ref["pb", i, m & ~(1 << i)], 0

    def put(level, p, m, r, c0, size, value):
        buf, first = source(level, p, m)
        side = sides[level] if level < blevels else side_of(m, level - blevels)
        buf[side, r, pl.ds(c0 - first, size), :] = value

    def rows(body):
        for g in range(groups):
            body(g)

    def tiles(p):
        found = [(c0_of[p], SUB, False)]
        if p == 0:
            found.insert(0, (block, halo_size, True))
        return found

    def normalise(p, m, c0, size, is_halo):
        nrm = ref["nrm", m]

        def body(g):
            out = []
            for i in range(SUB):
                r = g * SUB + i
                gain = nrm[1, pl.ds(r, 1), :]
                if is_halo:
                    part = ref["rawh", m][g, pl.ds(i, halo_chunks, stride=SUB), :]
                    if m == 0:
                        part = jnp.where(
                            k == sets - 1, hpeer[g, pl.ds(i, halo_chunks, stride=SUB), :], part,
                        )
                    gain = gain * keep
                else:
                    part = ref["raw", m, p][g, pl.ds(i, size, stride=SUB), :]
                out.append((part - nrm[0, pl.ds(r, 1), :]) * gain)
            for i in range(SUB):
                n = halo_chunks if is_halo else size
                ref["loc", 0, m][g * SUB + i, pl.ds(c0, n), :] = out[i]

        rows(body)

    def merged(low, high, lag, span, c0, size):
        if span < LANES:
            jump = 0
        else:
            jump = lag // LANES
            lag = lag % LANES
        cur = high(c0 + jump, size)
        nxt = high(c0 + jump + 1, size)
        lanes = lax.broadcasted_iota(jnp.int32, (size, LANES), 1)
        mixed = jnp.where(lanes < lag, nxt, cur)
        return low(c0, size) + pltpu.roll(mixed, (LANES - lag) % LANES, 1)

    def local_level(s, p, m, c0, size):
        span = 2**s
        src = ref["loc", s, m]
        table = ref["ld", m] if m else ld_ref

        def body(g):
            out = []
            for i in range(SUB):
                r = g * SUB + i
                base = (r // (2 * span)) * (2 * span)
                lo_row = base + table[0, s, r]
                hi_row = base + span + table[1, s, r]
                out.append(merged(
                    lambda c, n: src[lo_row, pl.ds(c, n), :],
                    lambda c, n: src[hi_row, pl.ds(c, n), :],
                    table[2, s, r], span, c0, size,
                ))
            for i in range(SUB):
                r = g * SUB + i
                if s + 1 < llevels:
                    ref["loc", s + 1, m][r, pl.ds(c0, size), :] = out[i]
                else:
                    put(0, p, m, r, c0, size, out[i])

        rows(body)

    def merge_level(j, p, m, c0, size):
        span = channels * 2**j
        src, first = source(j, p, m)
        table = ref["md", m] if m else md_ref

        def body(g):
            out = []
            for i in range(SUB):
                r = g * SUB + i
                lo_row = table[j, 0, r]
                hi_row = table[j, 1, r]
                out.append(merged(
                    lambda c, n: src[0, lo_row, pl.ds(c, n), :],
                    lambda c, n: src[1, hi_row, pl.ds(c, n), :],
                    table[j, 2, r], span, c0 - first, size,
                ))
            for i in range(SUB):
                r = g * SUB + i
                if j + 1 < flevels:
                    put(j + 1, p, m, r, c0, size, out[i])
                else:
                    fin[pl.ds(r * SUB, SUB), :] = out[i]

        rows(body)

    def prefix(m, c0):
        sums = jnp.dot(
            fin[...], tri[...], precision=lax.Precision.HIGHEST,
            preferred_element_type=jnp.float32,
        )
        own = sums[:, :LANES].reshape(channels, SUB, LANES)
        ref["eb", m][:, pl.ds(c0, SUB), :] = own
        return own, sums[:, LANES:].reshape(channels, SUB, LANES)

    def boxcar(p, m, c0):
        own, total = prefix(m, c0)
        far = total + ref["eb", m][:, pl.ds(c0 + 1, SUB), :]
        lanes = lax.broadcasted_iota(jnp.int32, (channels, SUB, LANES), 2)

        def body(at, best):
            for u in range(unroll):
                i = at * unroll + u
                wide = w_ref[i]
                mixed = jnp.where(lanes < wide, far, own)
                ahead = pltpu.roll(mixed, LANES - wide, 2)
                best = jnp.maximum(best, (ahead - own) * scl[i][None])
            return best

        unroll = math.gcd(nwidth, UNROLL)
        best = lax.fori_loop(
            0, nwidth // unroll, body, jnp.full((channels, SUB, LANES), -jnp.inf, jnp.float32)
        )
        for r in range(channels):
            g, i = r // SUB, r % SUB
            if m:
                ref["res", p, m][g, pl.ds(i, SUB, stride=SUB), :] = best[r]
            else:
                at = pl.multiple_of((k * block + c0) * SUB, SUB) + i
                o_ref[g, pl.ds(at, SUB, stride=SUB), :] = best[r]

    level_copies = {}
    for j in range(blevels):
        for p in range(count):
            for m in range(sets):
                size = SUB + (halo_chunks if p == 0 else 0)
                window = ref["bf", j, p, m].at[sides[j], :, pl.ds(0, size), :]
                level_copies[j, p, m] = push(
                    window, window, ref["bsend"].at[j, p, m], ref["brecv"].at[j, p, m], partners[j],
                )
    result_copies = {}
    for p in range(count):
        for m in remote:
            result_copies[p, m] = push(
                ref["res", p, m], o_ref.at[:, rows_of(k * block + c0_of[p], SUB), :],
                ref["osend"].at[p, m], ref["orecv"].at[p, m], same[m],
            )

    def local_stage(p, m):
        if m:
            if p == 0:
                for copy in [halo_copies[m], pack_copies[m]] + table_copies[m]:
                    copy.wait_recv()
                got = ref["pack", m][...]
                for g in range(groups):
                    for i in range(2):
                        at = (2 * g + i) * wide
                        ref["nrm", m][i, pl.ds(g * SUB, SUB), :] = jnp.broadcast_to(
                            got[:, at : at + 1], (SUB, LANES)
                        )
            raw_copies[p, m].wait_recv()
        else:
            if p == 0:
                own_halo.wait()
                peer_halo.wait_recv()
            own_loads[p].wait()
        for c0, size, is_halo in tiles(p):
            normalise(p, m, c0, size, is_halo)
            for s in range(llevels):
                local_level(s, p, m, c0, size)
        if blevels:
            level_copies[0, p, m].start()

    def merge_stage(j, p, m):
        if j < blevels:
            level_copies[j, p, m].wait_recv()
            if p:
                over = channels * 2**j // LANES + 1
                ref["bf", j, p, m][:, :, pl.ds(SUB, over), :] = ref["bf", j, p - 1, m][:, :, pl.ds(0, over), :]
        for c0, size, is_halo in tiles(p):
            if j + 1 < flevels:
                merge_level(j, p, m, c0, size)
            elif is_halo:
                merge_level(j, p, m, c0, SUB)
                prefix(m, c0)
            else:
                merge_level(j, p, m, c0, SUB)
                boxcar(p, m, c0)
        if j + 1 < blevels:
            level_copies[j + 1, p, m].start()
        if j + 1 == flevels and m:
            result_copies[p, m].start()

    if split == 0:
        lags = [FIRST_LAG] + [MID_LAG] * (flevels - 2) + [LAST_LAG]
        behind = [sum(lags[: j + 1]) for j in range(flevels)]
        for step in range(count + behind[-1]):
            if step < count:
                local_stage(step, 0)
            for j in range(flevels):
                if 0 <= step - behind[j] < count:
                    merge_stage(j, step - behind[j], 0)
    else:
        arrive = [m for m in LOCAL_ORDER if m < sets]
        leave = [m for m in LEAVE_ORDER if m < sets]
        local_stage(0, 0)
        local_stage(1, 0)
        for i, m in enumerate(arrive):
            local_stage(0, m)
            if i == INNER_AT:
                pl.when(jnp.logical_not(outer))(start_raw)
            if i == OUTER_AT:
                pl.when(outer)(start_raw)
        for p in range(count):
            for j in range(flevels - 1):
                for m in [0] + arrive:
                    merge_stage(j, p, m)
            for i, m in enumerate(leave):
                if i == NEXT_AT and p + 1 < count:
                    for n in arrive:
                        local_stage(p + 1, n)
                merge_stage(flevels - 1, p, m)
            if p + 2 < count:
                local_stage(p + 2, 0)
            merge_stage(flevels - 1, p, 0)

    for copy in result_copies.values():
        copy.wait_recv()
    for copy in sent:
        copy.wait_send()
LOCAL_ORDER = (1, 3, 2)
LEAVE_ORDER = (2, 3, 1)


def per_device(mesh_shape, spectra, local_delays, merge_delays, widths):
    channels, block_len = spectra.shape
    freq_count = mesh_shape["freq"]
    chunks = block_len // LANES
    groups = channels // SUB
    halo_chunks = -(-(channels * freq_count - 1 + LANES) // LANES)
    llevels = channels.bit_length() - 1
    flevels = freq_count.bit_length() - 1
    split = 0
    while (
        split < min(MAX_SPLIT, flevels)
        and chunks % (SUB * 2 ** (split + 2)) == 0
        and 4 * halo_chunks <= chunks // 2 ** (split + 1)
    ):
        split += 1
    sets = 2**split
    block = chunks // sets
    count = block // SUB
    blevels = flevels - split
    halo_size = -(-halo_chunks // SUB) * SUB
    over = -(-(channels * freq_count // 2 // LANES + 1) // SUB) * SUB
    depth = block + halo_size + SUB
    f32 = jnp.float32
    flat = spectra.reshape(groups, SUB, chunks, LANES).transpose(0, 2, 1, 3)
    flat = flat.reshape(groups, chunks * SUB, LANES)
    dma = pltpu.SemaphoreType.DMA

    def vmem(*shape):
        return pltpu.VMEM(shape, f32)

    scratch = {
        "xv": vmem(*flat.shape),
        "st_own": vmem(2, channels, LANES),
        "st_peer": vmem(2, channels, LANES),
        "pack": vmem(SUB, LANES),
        "hpeer": vmem(groups, halo_chunks * SUB, LANES),
        "fin": vmem(channels * SUB, LANES),
        "tri": vmem(LANES, 2 * LANES),
        "scl": vmem(widths.shape[0], SUB, LANES),
        "lsem": dma((2,)),
        "osem": dma((count,)),
        "psem": dma((4,)),
        "hsend": dma((sets,)),
        "hrecv": dma((sets,)),
        "ksend": dma((sets,)),
        "krecv": dma((sets,)),
        "tsend": dma((2, sets)),
        "trecv": dma((2, sets)),
        "rsend": dma((count, sets)),
        "rrecv": dma((count, sets)),
        "osend": dma((count, sets)),
        "orecv": dma((count, sets)),
        "ready": pltpu.SemaphoreType.REGULAR((sets,)),
    }
    if blevels:
        scratch["bsend"] = dma((blevels, count, sets))
        scratch["brecv"] = dma((blevels, count, sets))
    for m in range(sets):
        scratch["rawh", m] = vmem(groups, halo_chunks * SUB, LANES)
        scratch["nrm", m] = vmem(2, channels, LANES)
        scratch["eb", m] = vmem(channels, depth, LANES)
        for s in range(llevels):
            scratch["loc", s, m] = vmem(channels, depth, LANES)
        for p in range(count):
            scratch["raw", m, p] = vmem(groups, SUB * SUB, LANES)
            tail = (halo_size if p == 0 else 0) + over
            for j in range(blevels):
                scratch["bf", j, p, m] = vmem(2, channels, SUB + tail, LANES)
            if m:
                scratch["res", p, m] = vmem(groups, SUB * SUB, LANES)
        for i in range(split):
            if not (m >> i) & 1:
                scratch["pb", i, m] = vmem(2, channels, block + halo_size + over, LANES)
        if m:
            scratch["pack", m] = vmem(SUB, LANES)
            scratch["ld", m] = pltpu.SMEM((3, llevels, channels), jnp.int32)
            scratch["md", m] = pltpu.SMEM((flevels, 3, channels), jnp.int32)

    smem = pl.BlockSpec(memory_space=pltpu.SMEM)
    geo = (channels, chunks, freq_count, halo_chunks, split)
    out = pl.pallas_call(
        functools.partial(kernel, geo, tuple(scratch)),
        out_shape=pltpu.VMEM(flat.shape, f32),
        in_specs=[pl.BlockSpec(memory_space=pl.ANY), smem, smem, smem],
        out_specs=pl.BlockSpec(memory_space=pltpu.VMEM),
        scratch_shapes=list(scratch.values()),
        compiler_params=pltpu.CompilerParams(
            collective_id=0, has_side_effects=True, vmem_limit_bytes=56 * 2**20
        ),
    )(flat, local_delays.transpose(1, 0, 2), merge_delays, widths)
    out = out.reshape(groups, chunks, SUB, LANES).transpose(0, 2, 1, 3)
    return out.reshape(channels, block_len)


def solution(mesh):
    placed = (P(("beam", "freq"), "tm"), P(None, None, "freq"), P(None, None, "freq"), P())
    return jax.shard_map(
        functools.partial(per_device, dict(mesh.shape)), mesh=mesh, in_specs=placed,
        out_specs=P(("beam", "freq"), "tm"), check_vma=False,
    )
```

```python
import functools
import math

import jax
import jax.numpy as jnp
from jax import lax
from jax.experimental import pallas as pl
from jax.experimental.pallas import tpu as pltpu
from jax.sharding import PartitionSpec as P

WMAX = 32
EPSILON = 1e-05
LANES = 128
SUB = 8
MESH = pl.DeviceIdType.MESH
RAW_ORDER = (3, 2, 1)
LOCAL_ORDER = (1, 3, 2)
LEAVE_ORDER = (2, 3, 1)
DOWN_ORDER = (3, 2, 1)
DOWN_FIRST = 3
UP_ORDER = (1, 2, 3)
INNER_AT = -1
OUTER_AT = 2
NEXT_AT = 1
FIRST_LAG = 1
MID_LAG = 1
LAST_LAG = 3
UNROLL = 16
MAX_SPLIT = 2


def flip(value, mask):
    bit = 1
    while bit <= mask:
        if mask & bit:
            value = value + bit - 2 * bit * ((value // bit) % 2)
        bit *= 2
    return value


def kernel(geo, names, x_ref, ld_ref, md_ref, w_ref, o_ref, *scratch):
    channels, chunks, freq_count, halo_chunks, split = geo
    ref = dict(zip(names, scratch))
    sets = 2**split
    groups = channels // SUB
    llevels = channels.bit_length() - 1
    flevels = freq_count.bit_length() - 1
    blevels = flevels - split
    samples = chunks * LANES
    block = chunks // sets
    count = block // SUB
    lowest = freq_count // sets
    nwidth = w_ref.shape[0]
    xv, st_own, st_peer, pack, hpeer = (ref[n] for n in ("xv", "st_own", "st_peer", "pack", "hpeer"))
    fin, tri, scl = ref["fin"], ref["tri"], ref["scl"]

    tm = lax.axis_index("tm")
    freq = lax.axis_index("freq")
    k = freq // lowest
    f0 = freq % lowest
    peer = {"tm": 1 - tm}
    zs = [flip(k, m) for m in range(sets)]
    same = [{"freq": zs[m] * lowest + f0} for m in range(sets)]
    cross = [{"freq": zs[m] * lowest + f0, "tm": 1 - tm} for m in range(sets)]
    sides = [(freq // 2**j) % 2 for j in range(blevels)]
    partners = [{"freq": flip(freq, 2**j)} for j in range(blevels)]
    remote = [m for m in RAW_ORDER if m < sets] if sets > 1 else []

    barrier = pltpu.get_barrier_semaphore()
    for other in [peer] + partners:
        pl.semaphore_signal(barrier, inc=1, device_id=other, device_id_type=MESH)
    for m in remote:
        @pl.when(zs[m] > k)
        def _(m=m):
            for other in (same[m], cross[m]):
                pl.semaphore_signal(barrier, inc=1, device_id=other, device_id_type=MESH)

    c0_of = [block - SUB * (p + 1) for p in range(count)]

    def rows_of(first, size):
        return pl.ds(pl.multiple_of(first * SUB, SUB), size * SUB)

    load_x = pltpu.make_async_copy(x_ref, xv, ref["lsem"].at[0])
    load_x.start()
    own_loads = []
    for p in range(count):
        own_loads.append(pltpu.make_async_copy(
            x_ref.at[:, rows_of(k * block + c0_of[p], SUB), :], ref["raw", 0, p], ref["osem"].at[p],
        ))
    own_halo = pltpu.make_async_copy(
        x_ref.at[:, rows_of(jnp.minimum((k + 1) * block, chunks - halo_chunks), halo_chunks), :],
        ref["rawh", 0], ref["lsem"].at[1],
    )
    for copy in own_loads + [own_halo]:
        copy.start()

    sent = []

    def push(src, dst, ssem, rsem, device):
        copy = pltpu.make_async_remote_copy(
            src_ref=src, dst_ref=dst, send_sem=ssem, recv_sem=rsem,
            device_id=device, device_id_type=MESH,
        )
        sent.append(copy)
        return copy

    peer_halo = push(
        x_ref.at[:, pl.ds(0, halo_chunks * SUB), :], hpeer,
        ref["psem"].at[0], ref["psem"].at[1], peer,
    )
    stat_copy = push(st_own, st_peer, ref["psem"].at[2], ref["psem"].at[3], peer)
    raw_copies, halo_copies, pack_copies, table_copies = {}, {}, {}, {}
    for m in remote:
        last = zs[m] == sets - 1
        halo_copies[m] = push(
            x_ref.at[:, rows_of(jnp.where(last, 0, (zs[m] + 1) * block), halo_chunks), :],
            ref["rawh", m], ref["hsend"].at[m], ref["hrecv"].at[m],
            {"freq": zs[m] * lowest + f0, "tm": jnp.where(last, 1 - tm, tm)},
        )
        for p in range(count):
            raw_copies[p, m] = push(
                x_ref.at[:, rows_of(zs[m] * block + c0_of[p], SUB), :], ref["raw", m, p],
                ref["rsend"].at[p, m], ref["rrecv"].at[p, m], same[m],
            )
        pack_copies[m] = push(
            pack, ref["pack", m], ref["ksend"].at[m], ref["krecv"].at[m], same[m],
        )
        table_copies[m] = [
            push(ld_ref, ref["ld", m], ref["tsend"].at[0, m], ref["trecv"].at[0, m], same[m]),
            push(md_ref, ref["md", m], ref["tsend"].at[1, m], ref["trecv"].at[1, m], same[m]),
        ]

    pl.semaphore_wait(barrier, 1 + blevels + (2 * k if remote else 0))
    for m in remote:
        @pl.when(zs[m] < k)
        def _(m=m):
            for other in (same[m], cross[m]):
                pl.semaphore_signal(ref["ready"].at[m], inc=1, device_id=other, device_id_type=MESH)
    peer_halo.start()

    def start_tables(m):
        for copy in table_copies[m]:
            copy.start()

    def start_first(m):
        halo_copies[m].start()
        raw_copies[0, m].start()

    def at_distance(step, body):
        for m in remote:
            pl.when(zs[m] == k + step)(functools.partial(body, m))

    for step in DOWN_ORDER:
        at_distance(-step, start_tables)
    for step in DOWN_ORDER[:DOWN_FIRST]:
        at_distance(-step, start_first)
    outer = (k == 0) | (k == sets - 1)

    lane = lax.broadcasted_iota(jnp.int32, (SUB, LANES), 1)
    load_x.wait()
    for g in range(groups):
        data = xv[g].reshape(chunks, SUB, LANES)
        mean = jnp.sum(jnp.sum(data, axis=0), axis=1, keepdims=True) / samples
        off = data - mean[None]
        square = jnp.sum(jnp.sum(off * off, axis=0), axis=1, keepdims=True)
        st_own[0, pl.ds(g * SUB, SUB), :] = jnp.broadcast_to(mean, (SUB, LANES))
        st_own[1, pl.ds(g * SUB, SUB), :] = jnp.broadcast_to(square, (SUB, LANES))
    stat_copy.start()

    before = lax.broadcasted_iota(jnp.int32, (LANES, 2 * LANES), 0)
    after = lax.broadcasted_iota(jnp.int32, (LANES, 2 * LANES), 1)
    tri[...] = jnp.where(before < after, 1.0, 0.0)
    norm = 1.0 / math.sqrt(channels * freq_count)
    for i in range(nwidth):
        wide = jnp.full((SUB, LANES), w_ref[i].astype(jnp.float32), jnp.float32)
        scl[i] = (1.0 / jnp.sqrt(wide)) * norm

    stat_copy.wait_recv()
    mean_a, mean_b = st_own[0], st_peer[0]
    gap = mean_a - mean_b
    variance = (st_own[1] + st_peer[1] + gap * gap * (samples / 2)) / (2 * samples)
    mean_all = (mean_a + mean_b) * 0.5
    gain_all = 1.0 / jnp.sqrt(variance + EPSILON)
    ref["nrm", 0][0] = mean_all
    ref["nrm", 0][1] = gain_all
    wide = LANES // (2 * groups)
    packed = gain_all[(groups - 1) * SUB :]
    for g in reversed(range(groups)):
        if g < groups - 1:
            packed = jnp.where(lane < (2 * g + 2) * wide, gain_all[g * SUB : (g + 1) * SUB], packed)
        packed = jnp.where(lane < (2 * g + 1) * wide, mean_all[g * SUB : (g + 1) * SUB], packed)
    if remote:
        pack[...] = packed
    for step in DOWN_ORDER:
        at_distance(-step, lambda m: pack_copies[m].start())
    for step in DOWN_ORDER[DOWN_FIRST:]:
        at_distance(-step, start_first)

    def start_up(m):
        pl.semaphore_wait(ref["ready"].at[m], 2)
        start_tables(m)
        pack_copies[m].start()
        start_first(m)

    for step in UP_ORDER:
        at_distance(step, start_up)

    def start_raw():
        for p in range(1, count):
            for m in remote:
                raw_copies[p, m].start()

    if remote and INNER_AT < 0:
        pl.when(jnp.logical_not(outer))(start_raw)

    keep = jnp.where((tm == 1) & (k == sets - 1), 0.0, 1.0)
    halo_size = -(-halo_chunks // SUB) * SUB

    def side_of(m, i):
        bit = (k // 2**i) % 2
        return 1 - bit if (m >> i) & 1 else bit

    def source(level, p, m):
        if level < blevels:
            return ref["bf", level, p, m], c0_of[p]
        i = level - blevels
        return ref["pb", i, m & ~(1 << i)], 0

    def put(level, p, m, r, c0, size, value):
        buf, first = source(level, p, m)
        side = sides[level] if level < blevels else side_of(m, level - blevels)
        buf[side, r, pl.ds(c0 - first, size), :] = value

    def rows(body):
        for g in range(groups):
            body(g)

    def tiles(p):
        found = [(c0_of[p], SUB, False)]
        if p == 0:
            found.insert(0, (block, halo_size, True))
        return found

    def normalise(p, m, c0, size, is_halo):
        nrm = ref["nrm", m]

        def body(g):
            out = []
            for i in range(SUB):
                r = g * SUB + i
                gain = nrm[1, pl.ds(r, 1), :]
                if is_halo:
                    part = ref["rawh", m][g, pl.ds(i, halo_chunks, stride=SUB), :]
                    if m == 0:
                        part = jnp.where(
                            k == sets - 1, hpeer[g, pl.ds(i, halo_chunks, stride=SUB), :], part,
                        )
                    gain = gain * keep
                else:
                    part = ref["raw", m, p][g, pl.ds(i, size, stride=SUB), :]
                out.append((part - nrm[0, pl.ds(r, 1), :]) * gain)
            for i in range(SUB):
                n = halo_chunks if is_halo else size
                ref["loc", 0, m][g * SUB + i, pl.ds(c0, n), :] = out[i]

        rows(body)

    def merged(low, high, lag, span, c0, size):
        if span < LANES:
            jump = 0
        else:
            jump = lag // LANES
            lag = lag % LANES
        cur = high(c0 + jump, size)
        nxt = high(c0 + jump + 1, size)
        lanes = lax.broadcasted_iota(jnp.int32, (size, LANES), 1)
        mixed = jnp.where(lanes < lag, nxt, cur)
        return low(c0, size) + pltpu.roll(mixed, (LANES - lag) % LANES, 1)

    def local_level(s, p, m, c0, size):
        span = 2**s
        src = ref["loc", s, m]
        table = ref["ld", m] if m else ld_ref

        def body(g):
            out = []
            for i in range(SUB):
                r = g * SUB + i
                base = (r // (2 * span)) * (2 * span)
                lo_row = base + table[0, s, r]
                hi_row = base + span + table[1, s, r]
                out.append(merged(
                    lambda c, n: src[lo_row, pl.ds(c, n), :],
                    lambda c, n: src[hi_row, pl.ds(c, n), :],
                    table[2, s, r], span, c0, size,
                ))
            for i in range(SUB):
                r = g * SUB + i
                if s + 1 < llevels:
                    ref["loc", s + 1, m][r, pl.ds(c0, size), :] = out[i]
                else:
                    put(0, p, m, r, c0, size, out[i])

        rows(body)

    def merge_level(j, p, m, c0, size):
        span = channels * 2**j
        src, first = source(j, p, m)
        table = ref["md", m] if m else md_ref

        def body(g):
            out = []
            for i in range(SUB):
                r = g * SUB + i
                lo_row = table[j, 0, r]
                hi_row = table[j, 1, r]
                out.append(merged(
                    lambda c, n: src[0, lo_row, pl.ds(c, n), :],
                    lambda c, n: src[1, hi_row, pl.ds(c, n), :],
                    table[j, 2, r], span, c0 - first, size,
                ))
            for i in range(SUB):
                r = g * SUB + i
                if j + 1 < flevels:
                    put(j + 1, p, m, r, c0, size, out[i])
                else:
                    fin[pl.ds(r * SUB, SUB), :] = out[i]

        rows(body)

    def prefix(m, c0):
        sums = jnp.dot(
            fin[...], tri[...], precision=lax.Precision.HIGHEST,
            preferred_element_type=jnp.float32,
        )
        own = sums[:, :LANES].reshape(channels, SUB, LANES)
        ref["eb", m][:, pl.ds(c0, SUB), :] = own
        return own, sums[:, LANES:].reshape(channels, SUB, LANES)

    def boxcar(p, m, c0):
        own, total = prefix(m, c0)
        far = total + ref["eb", m][:, pl.ds(c0 + 1, SUB), :]
        lanes = lax.broadcasted_iota(jnp.int32, (channels, SUB, LANES), 2)

        def body(at, best):
            for u in range(unroll):
                i = at * unroll + u
                wide = w_ref[i]
                mixed = jnp.where(lanes < wide, far, own)
                ahead = pltpu.roll(mixed, LANES - wide, 2)
                best = jnp.maximum(best, (ahead - own) * scl[i][None])
            return best

        unroll = math.gcd(nwidth, UNROLL)
        best = lax.fori_loop(
            0, nwidth // unroll, body, jnp.full((channels, SUB, LANES), -jnp.inf, jnp.float32)
        )
        for r in range(channels):
            g, i = r // SUB, r % SUB
            if m:
                ref["res", p, m][g, pl.ds(i, SUB, stride=SUB), :] = best[r]
            else:
                at = pl.multiple_of((k * block + c0) * SUB, SUB) + i
                o_ref[g, pl.ds(at, SUB, stride=SUB), :] = best[r]

    level_copies = {}
    for j in range(blevels):
        for p in range(count):
            for m in range(sets):
                size = SUB + (halo_chunks if p == 0 else 0)
                window = ref["bf", j, p, m].at[sides[j], :, pl.ds(0, size), :]
                level_copies[j, p, m] = push(
                    window, window, ref["bsend"].at[j, p, m], ref["brecv"].at[j, p, m], partners[j],
                )
    result_copies = {}
    for p in range(count):
        for m in remote:
            result_copies[p, m] = push(
                ref["res", p, m], o_ref.at[:, rows_of(k * block + c0_of[p], SUB), :],
                ref["osend"].at[p, m], ref["orecv"].at[p, m], same[m],
            )

    def local_stage(p, m):
        if m:
            if p == 0:
                for copy in [halo_copies[m], pack_copies[m]] + table_copies[m]:
                    copy.wait_recv()
                got = ref["pack", m][...]
                for g in range(groups):
                    for i in range(2):
                        at = (2 * g + i) * wide
                        ref["nrm", m][i, pl.ds(g * SUB, SUB), :] = jnp.broadcast_to(
                            got[:, at : at + 1], (SUB, LANES)
                        )
            raw_copies[p, m].wait_recv()
        else:
            if p == 0:
                own_halo.wait()
                peer_halo.wait_recv()
            own_loads[p].wait()
        for c0, size, is_halo in tiles(p):
            normalise(p, m, c0, size, is_halo)
            for s in range(llevels):
                local_level(s, p, m, c0, size)
        if blevels:
            level_copies[0, p, m].start()

    def merge_stage(j, p, m):
        if j < blevels:
            level_copies[j, p, m].wait_recv()
            if p:
                over = channels * 2**j // LANES + 1
                ref["bf", j, p, m][:, :, pl.ds(SUB, over), :] = ref["bf", j, p - 1, m][:, :, pl.ds(0, over), :]
        for c0, size, is_halo in tiles(p):
            if j + 1 < flevels:
                merge_level(j, p, m, c0, size)
            elif is_halo:
                merge_level(j, p, m, c0, SUB)
                prefix(m, c0)
            else:
                merge_level(j, p, m, c0, SUB)
                boxcar(p, m, c0)
        if j + 1 < blevels:
            level_copies[j + 1, p, m].start()
        if j + 1 == flevels and m:
            result_copies[p, m].start()

    if split == 0:
        lags = [FIRST_LAG] + [MID_LAG] * (flevels - 2) + [LAST_LAG]
        behind = [sum(lags[: j + 1]) for j in range(flevels)]
        for step in range(count + behind[-1]):
            if step < count:
                local_stage(step, 0)
            for j in range(flevels):
                if 0 <= step - behind[j] < count:
                    merge_stage(j, step - behind[j], 0)
    else:
        arrive = [m for m in LOCAL_ORDER if m < sets]
        leave = [m for m in LEAVE_ORDER if m < sets]
        local_stage(0, 0)
        local_stage(1, 0)
        for i, m in enumerate(arrive):
            local_stage(0, m)
            if i == INNER_AT:
                pl.when(jnp.logical_not(outer))(start_raw)
            if i == OUTER_AT:
                pl.when(outer)(start_raw)
        for p in range(count):
            for j in range(blevels):
                for m in [0] + arrive:
                    merge_stage(j, p, m)
            built = set()

            def build(j, m):
                if (j, m) in built or j < blevels:
                    return
                built.add((j, m))
                if j > blevels:
                    build(j - 1, m & ~(1 << (j - blevels)))
                    build(j - 1, m | (1 << (j - blevels)))
                merge_stage(j, p, m)

            for i, m in enumerate(leave):
                if i == NEXT_AT and p + 1 < count:
                    for n in arrive:
                        local_stage(p + 1, n)
                build(flevels - 1, m)
            if p + 2 < count:
                local_stage(p + 2, 0)
            build(flevels - 1, 0)

    for copy in result_copies.values():
        copy.wait_recv()
    for copy in sent:
        copy.wait_send()

def per_device(mesh_shape, spectra, local_delays, merge_delays, widths):
    channels, block_len = spectra.shape
    freq_count = mesh_shape["freq"]
    chunks = block_len // LANES
    groups = channels // SUB
    halo_chunks = -(-(channels * freq_count - 1 + LANES) // LANES)
    llevels = channels.bit_length() - 1
    flevels = freq_count.bit_length() - 1
    split = 0
    while (
        split < min(MAX_SPLIT, flevels)
        and chunks % (SUB * 2 ** (split + 2)) == 0
        and 4 * halo_chunks <= chunks // 2 ** (split + 1)
    ):
        split += 1
    sets = 2**split
    block = chunks // sets
    count = block // SUB
    blevels = flevels - split
    halo_size = -(-halo_chunks // SUB) * SUB
    over = -(-(channels * freq_count // 2 // LANES + 1) // SUB) * SUB
    depth = block + halo_size + SUB
    f32 = jnp.float32
    flat = spectra.reshape(groups, SUB, chunks, LANES).transpose(0, 2, 1, 3)
    flat = flat.reshape(groups, chunks * SUB, LANES)
    dma = pltpu.SemaphoreType.DMA

    def vmem(*shape):
        return pltpu.VMEM(shape, f32)

    scratch = {
        "xv": vmem(*flat.shape),
        "st_own": vmem(2, channels, LANES),
        "st_peer": vmem(2, channels, LANES),
        "pack": vmem(SUB, LANES),
        "hpeer": vmem(groups, halo_chunks * SUB, LANES),
        "fin": vmem(channels * SUB, LANES),
        "tri": vmem(LANES, 2 * LANES),
        "scl": vmem(widths.shape[0], SUB, LANES),
        "lsem": dma((2,)),
        "osem": dma((count,)),
        "psem": dma((4,)),
        "hsend": dma((sets,)),
        "hrecv": dma((sets,)),
        "ksend": dma((sets,)),
        "krecv": dma((sets,)),
        "tsend": dma((2, sets)),
        "trecv": dma((2, sets)),
        "rsend": dma((count, sets)),
        "rrecv": dma((count, sets)),
        "osend": dma((count, sets)),
        "orecv": dma((count, sets)),
        "ready": pltpu.SemaphoreType.REGULAR((sets,)),
    }
    if blevels:
        scratch["bsend"] = dma((blevels, count, sets))
        scratch["brecv"] = dma((blevels, count, sets))
    for m in range(sets):
        scratch["rawh", m] = vmem(groups, halo_chunks * SUB, LANES)
        scratch["nrm", m] = vmem(2, channels, LANES)
        scratch["eb", m] = vmem(channels, depth, LANES)
        for s in range(llevels):
            scratch["loc", s, m] = vmem(channels, depth, LANES)
        for p in range(count):
            scratch["raw", m, p] = vmem(groups, SUB * SUB, LANES)
            tail = (halo_size if p == 0 else 0) + over
            for j in range(blevels):
                scratch["bf", j, p, m] = vmem(2, channels, SUB + tail, LANES)
            if m:
                scratch["res", p, m] = vmem(groups, SUB * SUB, LANES)
        for i in range(split):
            if not (m >> i) & 1:
                scratch["pb", i, m] = vmem(2, channels, block + halo_size + over, LANES)
        if m:
            scratch["pack", m] = vmem(SUB, LANES)
            scratch["ld", m] = pltpu.SMEM((3, llevels, channels), jnp.int32)
            scratch["md", m] = pltpu.SMEM((flevels, 3, channels), jnp.int32)

    smem = pl.BlockSpec(memory_space=pltpu.SMEM)
    geo = (channels, chunks, freq_count, halo_chunks, split)
    out = pl.pallas_call(
        functools.partial(kernel, geo, tuple(scratch)),
        out_shape=pltpu.VMEM(flat.shape, f32),
        in_specs=[pl.BlockSpec(memory_space=pl.ANY), smem, smem, smem],
        out_specs=pl.BlockSpec(memory_space=pltpu.VMEM),
        scratch_shapes=list(scratch.values()),
        compiler_params=pltpu.CompilerParams(
            collective_id=0, has_side_effects=True, vmem_limit_bytes=56 * 2**20
        ),
    )(flat, local_delays.transpose(1, 0, 2), merge_delays, widths)
    out = out.reshape(groups, chunks, SUB, LANES).transpose(0, 2, 1, 3)
    return out.reshape(channels, block_len)


def solution(mesh):
    placed = (P(("beam", "freq"), "tm"), P(None, None, "freq"), P(None, None, "freq"), P())
    return jax.shard_map(
        functools.partial(per_device, dict(mesh.shape)), mesh=mesh, in_specs=placed,
        out_specs=P(("beam", "freq"), "tm"), check_vma=False,
    )
```
